256 devices in a mesh: ctx: 64 (over z_lo, x, y), head: 4 (over z_hi, core).
Axes of the slice: x: 4, y: 4, z: 8 (z_hi: 2, z_lo: 4; z = z_hi * 4 + z_lo), core: 2. Of those that a mesh axis runs over, the one named last changes fastest.
Arguments:
- queries: bfloat16 [65536, 2048], P('ctx', 'head'), may hold values from -18 to 18
- keys: bfloat16 [65536, 2048], P('ctx', 'head'), may hold values from -6 to 6
- values: bfloat16 [65536, 2048], P('ctx', 'head'), may hold values from -6 to 6
- rates: float32 [65536, 4], P('ctx', 'head'), may hold values from 0.00017263349 to 0.0017263349
- fast_w1: bfloat16 [4, 512, 512], P('head'), may hold values from -0.25 to 0.25
- fast_w2: bfloat16 [4, 512, 512], P('head'), may hold values from -2 to 2
- fast_w3: bfloat16 [4, 512, 512], P('head'), may hold values from -0.25 to 0.25
- norm_gain: bfloat16 [2048], P('head'), may hold values from 0.25 to 1.75
- out_weight: bfloat16 [2048, 2048], P('head'), may hold values from -0.125 to 0.125
Outputs:
- output: bfloat16 [65536, 2048], P(('ctx', 'head'))
The draws below stay inside these ranges and needn't reach their ends.
All inputs are finite; a program needn't handle non-finite values.
Results may differ from the reference program's by a relative error of at most 0.014.
Values may be sent and summed in bfloat16 or wider, within the bound.
A program may use at most 64 MiB of HBM per device.

```python
import math
import jax
import jax.numpy as jnp
from jax import lax

D = 2048
HD = 512
HEADS = 4
WINDOW = 256
TOKENS = 65536


def pair_draw(key):
    folded = jax.random.fold_in(key, 11)
    query_seed, key_seed = jax.random.split(folded, 2)
    shape_all = (TOKENS, HEADS * HD)
    query_all = jnp.clip(jax.random.normal(query_seed, shape_all, jnp.float32), -6.0, 6.0)
    keys_all = jnp.clip(jax.random.normal(key_seed, shape_all, jnp.float32), -6.0, 6.0)
    return (query_all, keys_all)


def draw_queries(key, part):
    return pair_draw(key)[0].astype(jnp.bfloat16)


def draw_keys(key, part):
    return pair_draw(key)[1].astype(jnp.bfloat16)


def draw_fast_w2(key, part):
    folded = jax.random.fold_in(key, 23)
    head_scale = (1.0 + jnp.arange(HEADS, dtype=jnp.float32))[:, None, None] / math.sqrt(HD)
    values_raw = jnp.clip(jax.random.normal(folded, (HEADS, HD, HD), jnp.float32), -3.0, 3.0)
    return (values_raw * head_scale).astype(jnp.bfloat16)


def block_levels(rng, shape, cuts, low, largest):
    factor_of, own = 1.0, jax.random.fold_in(rng, 6)
    for position, blocks in cuts:
        steps = jnp.exp(jax.random.uniform(jax.random.fold_in(own, position), (blocks,), jnp.float32, low / len(cuts), largest / len(cuts)))
        factor_of = factor_of * jnp.repeat(steps, shape[position] // blocks).reshape([-1 if axis == position else 1 for axis in range(len(shape))])
    return factor_of


def bell_draw(rng, extent, spread, most, cuts=(), held_as=jnp.bfloat16):
    entries = jax.random.normal(rng, extent, jnp.float32) * spread
    if len(cuts) > 0:
        entries = block_levels(rng, extent, cuts, -0.22, 0.18) * entries
    return jnp.clip(entries, min=-most, max=most).astype(held_as)


def setup_inputs(seed: int = 0) -> dict:
    splits = jax.random.split(jax.random.key(seed), 10)
    return {
        "queries": draw_queries(jax.random.fold_in(splits[9], 71), 0),
        "keys": draw_keys(jax.random.fold_in(splits[9], 71), 0),
        "values": bell_draw(splits[2], (TOKENS, HEADS * HD), 1.0, 6.0, ((0, 64), (1, 4))),
        "rates": jnp.clip(jnp.exp(math.log(0.0017263349) - 2.3025851 * jax.random.uniform(splits[3], (TOKENS, HEADS), jnp.float32) ** block_levels(splits[3], (TOKENS, HEADS), ((0, 64), (1, 4)), -0.2, 0.2)), 0.00017263349, 0.0017263349),
        "fast_w1": bell_draw(splits[4], (HEADS, HD, HD), HD ** -0.5, 0.25, ((0, 4),)),
        "fast_w2": draw_fast_w2(jax.random.fold_in(splits[9], 71), 0),
        "fast_w3": bell_draw(splits[6], (HEADS, HD, HD), HD ** -0.5, 0.25, ((0, 4),)),
        "norm_gain": jnp.clip(1.0 + 0.15 * jax.random.normal(splits[7], (HEADS * HD,), jnp.float32), 0.25, 1.75).astype(jnp.bfloat16),
        "out_weight": bell_draw(splits[8], (HEADS * HD, D), (HEADS * HD) ** -0.5, 0.125, ((0, 4),)),
    }


EPSILON = 1e-06

def contract_rows(left_side, right_side):
    return lax.dot_general(left_side, right_side, (((0,), (0,)), ((), ())), preferred_element_type=jnp.float32)

def renorm(weight, push, axis_dim):
    widened = weight.astype(jnp.float32)
    updated = widened + push
    old_norm = jnp.sqrt(lax.optimization_barrier(jnp.mean(widened * widened, axis=axis_dim, keepdims=True)) + EPSILON)
    new_norm = jnp.sqrt(lax.optimization_barrier(jnp.mean(updated * updated, axis=axis_dim, keepdims=True)) + EPSILON)
    return (updated * (old_norm / new_norm)).astype(jnp.bfloat16)

def fast_pushes(key_rows, value_rows, rate_column, gate_weight, down_weight, up_weight):
    gate_part = jnp.dot(key_rows, gate_weight, preferred_element_type=jnp.float32)
    up_part = jnp.dot(key_rows, up_weight, preferred_element_type=jnp.float32)
    sigmoid_gate = jax.nn.sigmoid(gate_part)
    activation = (gate_part * sigmoid_gate * up_part).astype(jnp.bfloat16)
    scaled = (value_rows.astype(jnp.float32) * rate_column).astype(jnp.bfloat16)
    back_grad = lax.dot_general(scaled, down_weight, (((1,), (1,)), ((), ())), preferred_element_type=jnp.float32)
    grad_gate = (back_grad * up_part * sigmoid_gate * (1.0 + gate_part * (1.0 - sigmoid_gate))).astype(jnp.bfloat16)
    grad_up = (back_grad * gate_part * sigmoid_gate).astype(jnp.bfloat16)
    return (contract_rows(key_rows, grad_gate), contract_rows(activation, scaled), contract_rows(key_rows, grad_up))

def apply_fast(query_rows, gate_weight, down_weight, up_weight):
    gate_part = jnp.dot(query_rows, gate_weight, preferred_element_type=jnp.float32)
    up_part = jnp.dot(query_rows, up_weight, preferred_element_type=jnp.float32)
    mixed_act = (gate_part * jax.nn.sigmoid(gate_part) * up_part).astype(jnp.bfloat16)
    return jnp.dot(mixed_act, down_weight, preferred_element_type=jnp.float32)

def window_block(query_block, key_block, value_block, query_first, key_first):
    scores = lax.dot_general(query_block, key_block, (((1,), (1,)), ((), ())), preferred_element_type=jnp.float32)
    scores = scores * (1.0 / math.sqrt(query_block.shape[1]))
    query_pos = query_first + jnp.arange(query_block.shape[0], dtype=jnp.int32)
    key_pos = key_first + jnp.arange(key_block.shape[0], dtype=jnp.int32)
    allowed = (key_pos[None, :] <= query_pos[:, None]) & (key_pos[None, :] > query_pos[:, None] - WINDOW) & (key_pos[None, :] >= 0)
    scores = jnp.where(allowed, scores, -jnp.inf)
    row_peak = lax.optimization_barrier(jnp.max(scores, axis=1, keepdims=True))
    exponent = jnp.exp(scores - row_peak)
    weights = (exponent / lax.optimization_barrier(jnp.sum(exponent, axis=1, keepdims=True))).astype(jnp.bfloat16)
    return jnp.dot(weights, value_block, preferred_element_type=jnp.float32)

def window_head(query_rows, key_rows, value_rows):
    block_rows = min(512, TOKENS)
    padding = jnp.zeros((WINDOW, key_rows.shape[1]), key_rows.dtype)
    key_padded = jnp.concatenate([padding, key_rows], axis=0)
    value_padded = jnp.concatenate([padding, value_rows], axis=0)

    def one_block(block_index):
        first_row = (block_index * block_rows).astype(jnp.int32)
        query_block = lax.dynamic_slice_in_dim(query_rows, first_row, block_rows, 0)
        key_block = lax.dynamic_slice_in_dim(key_padded, first_row, block_rows + WINDOW, 0)
        value_block = lax.dynamic_slice_in_dim(value_padded, first_row, block_rows + WINDOW, 0)
        return window_block(query_block, key_block, value_block, first_row, first_row - WINDOW)
    stacked = lax.map(one_block, jnp.arange(TOKENS // block_rows, dtype=jnp.int32))
    return stacked.reshape(TOKENS, key_rows.shape[1])

def reference(queries, keys, values, rates, fast_w1, fast_w2, fast_w3, norm_gain, out_weight):
    head_outputs = []
    for head_index in range(HEADS):
        lower_col = head_index * HD
        upper_col = lower_col + HD
        query_rows = queries[:, lower_col:upper_col]
        key_rows = keys[:, lower_col:upper_col]
        value_rows = values[:, lower_col:upper_col]
        push_one, push_two, push_three = fast_pushes(key_rows, value_rows, rates[:, head_index:head_index + 1], fast_w1[head_index], fast_w2[head_index], fast_w3[head_index])
        new_gate = renorm(fast_w1[head_index], push_one, 0)
        new_down = renorm(fast_w2[head_index], push_two, 0)
        new_up = renorm(fast_w3[head_index], push_three, 0)
        fast_out = apply_fast(query_rows, new_gate, new_down, new_up)
        head_outputs.append(fast_out + window_head(query_rows, key_rows, value_rows))
    combined = jnp.concatenate(head_outputs, axis=1)
    mean_square = lax.optimization_barrier(jnp.mean(combined * combined, axis=1, keepdims=True))
    normed = (combined * lax.rsqrt(mean_square + EPSILON) * norm_gain.astype(jnp.float32)).astype(jnp.bfloat16)
    running = jnp.zeros((TOKENS, D), jnp.float32)
    for head_index in range(HEADS):
        lower_col = head_index * HD
        upper_col = lower_col + HD
        partial_out = jnp.dot(normed[:, lower_col:upper_col], out_weight[lower_col:upper_col], preferred_element_type=jnp.float32).astype(jnp.bfloat16)
        partial_out = lax.optimization_barrier(partial_out)
        running = running + partial_out.astype(jnp.float32)
    return running.astype(jnp.bfloat16)
```

```python
import math

import jax
import jax.numpy as jnp
from jax import lax
from jax.experimental import pallas as pl
from jax.experimental.pallas import tpu as pltpu
from jax.sharding import PartitionSpec as P

MESH = pl.DeviceIdType.MESH
WINDOW = 256
EPSILON = 1e-06
TOK = 1024
HD = 512
DM = 2048
NEG = -1e30
BF = jnp.bfloat16
F32 = jnp.float32


def dotf(a, b, ca=1, cb=0):
    return lax.dot_general(a, b, (((ca,), (cb,)), ((), ())), preferred_element_type=F32)


def device(zl, x, y, zh, core):
    return (zl * 16 + x * 4 + y, zh * 2 + core)


def aligned(value, by):
    return pl.multiple_of(value, by)


def layer_kernel(
    q_ref, k_ref, v_ref, rate_ref, w1_ref, w2_ref, w3_ref, gain_ref, ow_ref, o_ref,
    kx, vx, qv, w, rb, act, sc, g1, g3, ps, r1, q2, r2, q3, r3, f, asum, win, wo, cs, cr, acc, gains,
    send_sem, recv_sem, local_sem,
):
    c = lax.axis_index("ctx")
    h = lax.axis_index("head")
    zl, x, y = c // 16, (c // 4) % 4, c % 4
    zh, core = h // 2, h % 2

    def at_x(d):
        return device(zl, (x + d) % 4, y, zh, core)

    def at_y(d):
        return device(zl, x, (y + d) % 4, zh, core)

    def at_z(d):
        return device((zl + d) % 4, x, y, zh, core)

    def at_head(other_z, other_core):
        return device(
            zl, x, y, (zh + other_z) % 2, (core + other_core) % 2
        )

    following = ((c + 1) % 64, h)
    previous = ((c + 63) % 64, h)
    mirror = device(3 - zl, x, y, 1 - zh, core)
    used = [0]
    sends = []

    def put(src, dst, to):
        index = used[0]
        used[0] += 1
        copy = pltpu.make_async_remote_copy(
            src_ref=src, dst_ref=dst, send_sem=send_sem.at[index], recv_sem=recv_sem.at[index],
            device_id=to, device_id_type=MESH,
        )
        copy.start()
        sends.append(copy)
        return copy

    local = []

    def fetch(src, dst):
        copy = pltpu.make_async_copy(src, dst, local_sem.at[len(local)])
        copy.start()
        local.append(copy)
        return copy

    first = [
        fetch(k_ref, kx.at[pl.ds(WINDOW, TOK)]),
        fetch(w1_ref, w.at[0]),
        fetch(w3_ref, w.at[2]),
        fetch(v_ref, vx.at[pl.ds(WINDOW, TOK)]),
        fetch(w2_ref, w.at[1]),
    ]
    get_q = fetch(q_ref, qv)
    own_rows = pl.ds(aligned(h * HD, HD), HD)
    get_wo = fetch(ow_ref, wo.at[own_rows])
    get_gain = fetch(gain_ref, gains.at[h])

    barrier = pltpu.get_barrier_semaphore()
    peers = [at_x(d) for d in (1, 2, 3)] + [at_y(d) for d in (1, 2, 3)] + [at_z(d) for d in (1, 2, 3)]
    peers += [at_head(0, 1), at_head(1, 0), at_head(1, 1), following, previous, mirror]
    for peer in peers:
        pl.semaphore_signal(barrier, inc=1, device_id=peer, device_id_type=MESH)
    pl.semaphore_wait(barrier, len(peers))

    halo = [
        put(k_ref.at[pl.ds(TOK - WINDOW, WINDOW)], kx.at[pl.ds(0, WINDOW)], following),
        put(v_ref.at[pl.ds(TOK - WINDOW, WINDOW)], vx.at[pl.ds(0, WINDOW)], following),
    ]
    row_a = aligned(x * 128 + y * 32, 32)
    row_b = aligned(y * 128 + x * 32, 32)
    crossed = [
        put(
            ow_ref.at[pl.ds(row, 32), pl.ds(col, 1024)],
            wo.at[pl.ds(aligned(h * HD + row, 32), 32), pl.ds(col, 1024)],
            mirror,
        )
        for row, col in ((row_a, 0), (row_b, 1024))
    ]
    own_core = [put(ow_ref, wo.at[own_rows], at_head(0, 1))]
    gain_got = [put(gain_ref, gains.at[h], at_head(a, b)) for a, b in ((0, 1), (1, 0), (1, 1))]

    for group in range(8):
        row = jnp.broadcast_to(rate_ref[group : group + 1, :], (128, 128))
        rb[group * 128 : (group + 1) * 128, :] = jnp.transpose(row)
    for copy in first:
        copy.wait()

    def token_block(i, carry):
        rows = pl.ds(aligned(i * 256, 256), 256)
        ext = pl.ds(aligned(i * 256 + WINDOW, 256), 256)
        key_rows = kx[ext, :]
        gate = dotf(key_rows, w[0])
        up = dotf(key_rows, w[2])
        sig = jax.nn.sigmoid(gate)
        gated = gate * sig
        act[rows, :] = (gated * up).astype(BF)
        rate = rb[rows, :]
        scaled = (vx[ext, :].astype(F32) * jnp.concatenate([rate] * 4, axis=1)).astype(BF)
        sc[rows, :] = scaled
        back = dotf(scaled, w[1], 1, 1)
        g1[rows, :] = (back * up * sig * (1.0 + gate * (1.0 - sig))).astype(BF)
        g3[rows, :] = (back * gated).astype(BF)
        return carry

    lax.fori_loop(0, TOK // 256, token_block, 0)

    own_keys = pl.ds(WINDOW, TOK)
    s1 = []
    for m in (1, 0, 2):
        for block in range(4):
            cols = pl.ds(block * 128, 128)
            left = act[:, cols] if m == 1 else kx[own_keys, cols]
            right = (g1, sc, g3)[m][...]
            ps[m, block * 128 : (block + 1) * 128, :] = dotf(left, right, 0, 0).astype(BF)
        got = []
        for d in (1, 2, 3):
            to_x = pl.ds(aligned(((x + d) % 4) * 128, 128), 128)
            to_y = pl.ds(aligned(((y + d) % 4) * 128, 128), 128)
            got.append(put(ps.at[m, to_x, pl.ds(0, 256)], r1.at[0, d - 1, m], at_x(d)))
            got.append(put(ps.at[m, to_y, pl.ds(256, 256)], r1.at[1, d - 1, m], at_y(d)))
        s1.append((m, got))

    def window_block(b):
        queries = qv[b * 256 : (b + 1) * 256, :]
        scores = dotf(queries, kx[b * 256 : b * 256 + 512, :], 1, 1) * (1.0 / math.sqrt(HD))
        qi = lax.broadcasted_iota(jnp.int32, (256, 512), 0)
        ki = lax.broadcasted_iota(jnp.int32, (256, 512), 1)
        allowed = (ki <= qi + WINDOW) & (ki > qi)
        if b == 0:
            allowed = allowed & (ki >= jnp.where(c == 0, WINDOW, 0))
        scores = jnp.where(allowed, scores, NEG)
        peak = jnp.max(scores, axis=1, keepdims=True)
        expo = jnp.where(allowed, jnp.exp(scores - peak), 0.0)
        weights = (expo / jnp.sum(expo, axis=1, keepdims=True)).astype(BF)
        win[b * 256 : (b + 1) * 256, :] = dotf(weights, vx[b * 256 : b * 256 + 512, :])

    get_q.wait()
    for m in range(3):
        wide = w[m].astype(F32)
        asum[m : m + 1, :] = jnp.sum(wide * wide, axis=0, keepdims=True)
    window_block(1)
    window_block(2)
    for copy in halo:
        copy.wait_recv()

    s2 = []
    for turn, (m, got) in enumerate(s1):
        if turn < 2:
            window_block((3, 0)[turn])
        for copy in got:
            copy.wait_recv()
        own_x = pl.ds(aligned(x * 128, 128), 128)
        own_y = pl.ds(aligned(y * 128, 128), 128)
        for half, own in ((0, own_x), (1, own_y)):
            total = ps[m, own, half * 256 : (half + 1) * 256].astype(F32)
            for d in range(3):
                total = total + r1[half, d, m].astype(F32)
            q2[half, m] = total.astype(BF)
        nxt = []
        for d in (1, 2, 3):
            to_y = pl.ds(aligned(((y + d) % 4) * 32, 32), 32)
            to_x = pl.ds(aligned(((x + d) % 4) * 32, 32), 32)
            nxt.append(put(q2.at[0, m, to_y], r2.at[0, d - 1, m], at_y(d)))
            nxt.append(put(q2.at[1, m, to_x], r2.at[1, d - 1, m], at_x(d)))
        s2.append((m, nxt))
    for m, got in s2:
        for copy in got:
            copy.wait_recv()
        own_y = pl.ds(aligned(y * 32, 32), 32)
        own_x = pl.ds(aligned(x * 32, 32), 32)
        for half, own in ((0, own_y), (1, own_x)):
            total = q2[half, m, own, :].astype(F32)
            for d in range(3):
                total = total + r2[half, d, m].astype(F32)
            q3[2 * half, m] = total[:, :128].astype(BF)
            q3[2 * half + 1, m] = total[:, 128:].astype(BF)
    s3 = [put(q3.at[(zl + d) % 4], r3.at[d - 1], at_z(d)) for d in (1, 2, 3)]
    for copy in s3:
        copy.wait_recv()
    flip = zl // 2
    row_z = pl.ds(aligned((1 - flip) * row_a + flip * row_b, 32), 32)
    col_z = pl.ds(aligned(zl * 128, 128), 128)
    for m in range(3):
        total = q3[zl, m].astype(F32)
        for d in range(3):
            total = total + r3[d, m].astype(F32)
        f[m, row_z, col_z] = total.astype(BF)

    mine = f.at[:, row_z, col_z]
    for copy in [put(mine, mine, at_z(d)) for d in (1, 2, 3)]:
        copy.wait_recv()
    part_a = f.at[:, pl.ds(row_a, 32), pl.ds(0, 256)]
    part_b = f.at[:, pl.ds(row_b, 32), pl.ds(256, 256)]
    s5 = []
    for d in (1, 2, 3):
        s5.append(put(part_a, part_a, at_y(d)))
        s5.append(put(part_b, part_b, at_x(d)))
    for copy in s5:
        copy.wait_recv()
    s6 = []
    for m in (0, 2, 1):
        part_a = f.at[m, pl.ds(aligned(x * 128, 128), 128), pl.ds(0, 256)]
        part_b = f.at[m, pl.ds(aligned(y * 128, 128), 128), pl.ds(256, 256)]
        got = []
        for d in (1, 2, 3):
            got.append(put(part_a, part_a, at_x(d)))
            got.append(put(part_b, part_b, at_y(d)))
        s6.append((m, got))

    h_far = (1 - zh) * 2 + core
    base = h_far * HD
    for copy in crossed:
        copy.wait_recv()
    part_a = wo.at[pl.ds(aligned(base + row_a, 32), 32), pl.ds(0, 1024)]
    part_b = wo.at[pl.ds(aligned(base + row_b, 32), 32), pl.ds(1024, 1024)]
    spread = []
    for d in (1, 2, 3):
        spread.append(put(part_a, part_a, at_y(d)))
        spread.append(put(part_b, part_b, at_x(d)))

    for m, got in s6:
        for copy in got:
            copy.wait_recv()
        updated = w[m].astype(F32) + f[m].astype(F32)
        new_mean = jnp.sum(updated * updated, axis=0, keepdims=True) * (1.0 / HD)
        old_mean = asum[m : m + 1, :] * (1.0 / HD)
        ratio = jnp.sqrt(old_mean + EPSILON) / jnp.sqrt(new_mean + EPSILON)
        w[m] = (updated * ratio).astype(BF)

    for copy in spread:
        copy.wait_recv()
    part_a = wo.at[pl.ds(aligned(base + x * 128, 128), 128), pl.ds(0, 1024)]
    part_b = wo.at[pl.ds(aligned(base + y * 128, 128), 128), pl.ds(1024, 1024)]
    spread = []
    for d in (1, 2, 3):
        spread.append(put(part_a, part_a, at_x(d)))
        spread.append(put(part_b, part_b, at_y(d)))

    arrived = []
    for far, other in ((1, 0), (1, 1), (0, 1), (0, 0)):
        target = ((zh + far) % 2) * 2 + (core + other) % 2
        rows = pl.ds(aligned(target * 256, 256), 256)
        queries = qv[rows, :]
        gate = dotf(queries, w[0])
        up = dotf(queries, w[2])
        mixed = (gate * jax.nn.sigmoid(gate) * up).astype(BF)
        combined = (dotf(mixed, w[1]) + win[rows, :]).astype(BF)
        if far or other:
            cs[rows, :] = combined
            arrived.append((far, other, put(cs.at[rows], cr.at[h], at_head(far, other))))
        else:
            cr[h] = combined

    for copy in own_core + gain_got:
        copy.wait_recv()
    get_gain.wait()
    get_wo.wait()

    def project(far, other, fresh, squares):
        source = ((zh + far) % 2) * 2 + (core + other) % 2
        wide = cr[source].astype(F32)
        squares = squares + jnp.sum(wide * wide, axis=1, keepdims=True)
        gained = (wide * gains[source][0:1, :]).astype(BF)
        rows = pl.ds(aligned(source * HD, HD), HD)
        for n in range(4):
            cols = pl.ds(n * 512, 512)
            part = dotf(gained, wo[rows, cols])
            acc[:, cols] = part if fresh else acc[:, cols] + part
        return squares

    squares = project(0, 0, True, jnp.zeros((256, 1), F32))
    arrived[2][2].wait_recv()
    squares = project(0, 1, False, squares)
    for copy in spread:
        copy.wait_recv()
    far_rows = pl.ds(aligned(base, HD), HD)
    shared = put(wo.at[far_rows], wo.at[far_rows], at_head(0, 1))
    arrived[0][2].wait_recv()
    squares = project(1, 0, False, squares)
    arrived[1][2].wait_recv()
    shared.wait_recv()
    squares = project(1, 1, False, squares)
    scale = lax.rsqrt(squares * (1.0 / DM) + EPSILON)
    o_ref[...] = (acc[...] * scale).astype(BF)
    for copy in sends:
        copy.wait_send()


def body(queries, keys, values, rates, fast_w1, fast_w2, fast_w3, norm_gain, out_weight):
    gain = jnp.broadcast_to(norm_gain.astype(F32)[None, :], (8, HD))
    anywhere = pl.BlockSpec(memory_space=pl.ANY)
    vmem = pl.BlockSpec(memory_space=pltpu.VMEM)
    n_copies = 96
    return pl.pallas_call(
        layer_kernel,
        out_shape=jax.ShapeDtypeStruct((TOK // 4, DM), BF),
        in_specs=[anywhere, anywhere, anywhere, vmem, anywhere, anywhere, anywhere, anywhere, anywhere],
        out_specs=vmem,
        scratch_shapes=[
            pltpu.VMEM((WINDOW + TOK, HD), BF),
            pltpu.VMEM((WINDOW + TOK, HD), BF),
            pltpu.VMEM((TOK, HD), BF),
            pltpu.VMEM((3, HD, HD), BF),
            pltpu.VMEM((TOK, 128), F32),
            pltpu.VMEM((TOK, HD), BF),
            pltpu.VMEM((TOK, HD), BF),
            pltpu.VMEM((TOK, HD), BF),
            pltpu.VMEM((TOK, HD), BF),
            pltpu.VMEM((3, HD, HD), BF),
            pltpu.VMEM((2, 3, 3, 128, 256), BF),
            pltpu.VMEM((2, 3, 128, 256), BF),
            pltpu.VMEM((2, 3, 3, 32, 256), BF),
            pltpu.VMEM((4, 3, 32, 128), BF),
            pltpu.VMEM((3, 3, 32, 128), BF),
            pltpu.VMEM((3, HD, HD), BF),
            pltpu.VMEM((8, HD), F32),
            pltpu.VMEM((TOK, HD), F32),
            pltpu.VMEM((DM, DM), BF),
            pltpu.VMEM((TOK, HD), BF),
            pltpu.VMEM((4, 256, HD), BF),
            pltpu.VMEM((256, DM), F32),
            pltpu.VMEM((4, 8, HD), F32),
            pltpu.SemaphoreType.DMA((n_copies,)),
            pltpu.SemaphoreType.DMA((n_copies,)),
            pltpu.SemaphoreType.DMA((8,)),
        ],
        name="layer",
        compiler_params=pltpu.CompilerParams(
            collective_id=0, has_side_effects=True, vmem_limit_bytes=56 << 20
        ),
    )(
        queries, keys, values, rates.reshape(8, 128),
        fast_w1[0], fast_w2[0], fast_w3[0], gain, out_weight,
    )


def solution(mesh):
    placed = (
        P("ctx", "head"),
        P("ctx", "head"),
        P("ctx", "head"),
        P("ctx", "head"),
        P("head", None, None),
        P("head", None, None),
        P("head", None, None),
        P("head"),
        P("head", None),
    )
    return jax.shard_map(
        body, mesh=mesh, in_specs=placed, out_specs=P(("ctx", "head"), None), check_vma=False
    )
```

```python
import math

import jax
import jax.numpy as jnp
from jax import lax
from jax.experimental import pallas as pl
from jax.experimental.pallas import tpu as pltpu
from jax.sharding import PartitionSpec as P

MESH = pl.DeviceIdType.MESH
WINDOW = 256
EPSILON = 1e-06
TOK = 1024
HD = 512
DM = 2048
NEG = -1e30
BF = jnp.bfloat16
F32 = jnp.float32


def dotf(a, b, ca=1, cb=0):
    return lax.dot_general(a, b, (((ca,), (cb,)), ((), ())), preferred_element_type=F32)


def device(zl, x, y, zh, core):
    return (zl * 16 + x * 4 + y, zh * 2 + core)


def aligned(value, by):
    return pl.multiple_of(value, by)


def layer_kernel(
    q_ref, k_ref, v_ref, rate_ref, w1_ref, w2_ref, w3_ref, gain_ref, ow_ref, o_ref,
    kx, vx, qv, w, rb, act, sc, g1, g3, ps, r1, q2, r2, q3, r3, f, asum, win, wo, cs, cr, acc, gains,
    send_sem, recv_sem, local_sem,
):
    c = lax.axis_index("ctx")
    h = lax.axis_index("head")
    zl, x, y = c // 16, (c // 4) % 4, c % 4
    zh, core = h // 2, h % 2

    def at_x(d):
        return device(zl, (x + d) % 4, y, zh, core)

    def at_y(d):
        return device(zl, x, (y + d) % 4, zh, core)

    def at_z(d):
        return device((zl + d) % 4, x, y, zh, core)

    def at_head(other_z, other_core):
        return device(
            zl, x, y, (zh + other_z) % 2, (core + other_core) % 2
        )

    following = ((c + 1) % 64, h)
    previous = ((c + 63) % 64, h)
    mirror = device(3 - zl, x, y, 1 - zh, core)
    used = [0]
    sends = []

    def put(src, dst, to):
        index = used[0]
        used[0] += 1
        copy = pltpu.make_async_remote_copy(
            src_ref=src, dst_ref=dst, send_sem=send_sem.at[index], recv_sem=recv_sem.at[index],
            device_id=to, device_id_type=MESH,
        )
        copy.start()
        sends.append(copy)
        return copy

    local = []

    def fetch(src, dst):
        copy = pltpu.make_async_copy(src, dst, local_sem.at[len(local)])
        copy.start()
        local.append(copy)
        return copy

    first = [
        fetch(k_ref, kx.at[pl.ds(WINDOW, TOK)]),
        fetch(w1_ref, w.at[0]),
        fetch(w3_ref, w.at[2]),
        fetch(v_ref, vx.at[pl.ds(WINDOW, TOK)]),
        fetch(w2_ref, w.at[1]),
    ]
    get_q = fetch(q_ref, qv)
    own_rows = pl.ds(aligned(h * HD, HD), HD)
    get_wo = fetch(ow_ref, wo.at[own_rows])
    get_gain = fetch(gain_ref, gains.at[h])

    barrier = pltpu.get_barrier_semaphore()
    peers = [at_x(d) for d in (1, 2, 3)] + [at_y(d) for d in (1, 2, 3)] + [at_z(d) for d in (1, 2, 3)]
    peers += [at_head(0, 1), at_head(1, 0), at_head(1, 1), following, previous, mirror]
    for peer in peers:
        pl.semaphore_signal(barrier, inc=1, device_id=peer, device_id_type=MESH)

    for group in range(8):
        row = jnp.broadcast_to(rate_ref[group : group + 1, :], (128, 128))
        rb[group * 128 : (group + 1) * 128, :] = jnp.transpose(row)
    for copy in first:
        copy.wait()

    def token_block(i, carry):
        rows = pl.ds(aligned(i * 256, 256), 256)
        ext = pl.ds(aligned(i * 256 + WINDOW, 256), 256)
        key_rows = kx[ext, :]
        gate = dotf(key_rows, w[0])
        up = dotf(key_rows, w[2])
        sig = jax.nn.sigmoid(gate)
        gated = gate * sig
        act[rows, :] = (gated * up).astype(BF)
        rate = rb[rows, :]
        scaled = (vx[ext, :].astype(F32) * jnp.concatenate([rate] * 4, axis=1)).astype(BF)
        sc[rows, :] = scaled
        back = dotf(scaled, w[1], 1, 1)
        g1[rows, :] = (back * up * sig * (1.0 + gate * (1.0 - sig))).astype(BF)
        g3[rows, :] = (back * gated).astype(BF)
        return carry

    lax.fori_loop(0, 1, token_block, 0)
    pl.semaphore_wait(barrier, len(peers))

    tail = pl.ds(TOK - WINDOW, WINDOW)
    head = pl.ds(0, WINDOW)
    halo = [put(k_ref.at[tail], kx.at[head], following)]
    row_a = aligned(x * 128 + y * 32, 32)
    row_b = aligned(y * 128 + x * 32, 32)
    gain_got = [put(gain_ref, gains.at[h], at_head(a, b)) for a, b in ((0, 1), (1, 0), (1, 1))]
    lax.fori_loop(1, TOK // 256, token_block, 0)

    order = (0, 2, 1)
    own_keys = pl.ds(WINDOW, TOK)
    s1, s2, s3, s4, s5, s6 = {}, {}, {}, {}, {}, {}
    for m in order:
        for block in range(4):
            cols = pl.ds(block * 128, 128)
            left = act[:, cols] if m == 1 else kx[own_keys, cols]
            right = (g1, sc, g3)[m][...]
            ps[m, block * 128 : (block + 1) * 128, :] = dotf(left, right, 0, 0).astype(BF)
        s1[m] = []
        for d in (1, 2, 3):
            to_x = pl.ds(aligned(((x + d) % 4) * 128, 128), 128)
            to_y = pl.ds(aligned(((y + d) % 4) * 128, 128), 128)
            s1[m].append(put(ps.at[m, to_x, pl.ds(0, 256)], r1.at[0, d - 1, m], at_x(d)))
            s1[m].append(put(ps.at[m, to_y, pl.ds(256, 256)], r1.at[1, d - 1, m], at_y(d)))
    crossed = [
        put(
            ow_ref.at[pl.ds(row, 32), pl.ds(col, 1024)],
            wo.at[pl.ds(aligned(h * HD + row, 32), 32), pl.ds(col, 1024)],
            mirror,
        )
        for row, col in ((row_a, 0), (row_b, 1024))
    ]

    def window_block(b):
        queries = qv[b * 256 : (b + 1) * 256, :]
        scores = dotf(queries, kx[b * 256 : b * 256 + 512, :], 1, 1) * (1.0 / math.sqrt(HD))
        qi = lax.broadcasted_iota(jnp.int32, (256, 512), 0)
        ki = lax.broadcasted_iota(jnp.int32, (256, 512), 1)
        allowed = (ki <= qi + WINDOW) & (ki > qi)
        if b == 0:
            allowed = allowed & (ki >= jnp.where(c == 0, WINDOW, 0))
        scores = jnp.where(allowed, scores, NEG)
        peak = jnp.max(scores, axis=1, keepdims=True)
        expo = jnp.where(allowed, jnp.exp(scores - peak), 0.0)
        weights = (expo / jnp.sum(expo, axis=1, keepdims=True)).astype(BF)
        win[b * 256 : (b + 1) * 256, :] = dotf(weights, vx[b * 256 : b * 256 + 512, :])

    get_q.wait()
    for m in range(3):
        wide = w[m].astype(F32)
        asum[m : m + 1, :] = jnp.sum(wide * wide, axis=0, keepdims=True)

    def all_of(copies):
        for copy in copies:
            copy.wait_recv()

    def stage_two(m):
        all_of(s1[m])
        own_x = pl.ds(aligned(x * 128, 128), 128)
        own_y = pl.ds(aligned(y * 128, 128), 128)
        for half, own in ((0, own_x), (1, own_y)):
            total = ps[m, own, half * 256 : (half + 1) * 256].astype(F32)
            for d in range(3):
                total = total + r1[half, d, m].astype(F32)
            q2[half, m] = total.astype(BF)
        s2[m] = []
        for d in (1, 2, 3):
            to_y = pl.ds(aligned(((y + d) % 4) * 32, 32), 32)
            to_x = pl.ds(aligned(((x + d) % 4) * 32, 32), 32)
            s2[m].append(put(q2.at[0, m, to_y], r2.at[0, d - 1, m], at_y(d)))
            s2[m].append(put(q2.at[1, m, to_x], r2.at[1, d - 1, m], at_x(d)))

    def stage_three(m):
        all_of(s2[m])
        own_y = pl.ds(aligned(y * 32, 32), 32)
        own_x = pl.ds(aligned(x * 32, 32), 32)
        for half, own in ((0, own_y), (1, own_x)):
            total = q2[half, m, own, :].astype(F32)
            for d in range(3):
                total = total + r2[half, d, m].astype(F32)
            q3[2 * half, m] = total[:, :128].astype(BF)
            q3[2 * half + 1, m] = total[:, 128:].astype(BF)
        s3[m] = [put(q3.at[(zl + d) % 4, m], r3.at[d - 1, m], at_z(d)) for d in (1, 2, 3)]

    flip = zl // 2
    row_z = pl.ds(aligned((1 - flip) * row_a + flip * row_b, 32), 32)
    col_z = pl.ds(aligned(zl * 128, 128), 128)

    def stage_four(m):
        all_of(s3[m])
        total = q3[zl, m].astype(F32)
        for d in range(3):
            total = total + r3[d, m].astype(F32)
        f[m, row_z, col_z] = total.astype(BF)
        mine = f.at[m, row_z, col_z]
        s4[m] = [put(mine, mine, at_z(d)) for d in (1, 2, 3)]

    def stage_five(m):
        all_of(s4[m])
        part_a = f.at[m, pl.ds(row_a, 32), pl.ds(0, 256)]
        part_b = f.at[m, pl.ds(row_b, 32), pl.ds(256, 256)]
        s5[m] = []
        for d in (1, 2, 3):
            s5[m].append(put(part_a, part_a, at_y(d)))
            s5[m].append(put(part_b, part_b, at_x(d)))

    def stage_six(m):
        all_of(s5[m])
        part_a = f.at[m, pl.ds(aligned(x * 128, 128), 128), pl.ds(0, 256)]
        part_b = f.at[m, pl.ds(aligned(y * 128, 128), 128), pl.ds(256, 256)]
        s6[m] = []
        for d in (1, 2, 3):
            s6[m].append(put(part_a, part_a, at_x(d)))
            s6[m].append(put(part_b, part_b, at_y(d)))

    def renew(m):
        all_of(s6[m])
        updated = w[m].astype(F32) + f[m].astype(F32)
        new_mean = jnp.sum(updated * updated, axis=0, keepdims=True) * (1.0 / HD)
        old_mean = asum[m : m + 1, :] * (1.0 / HD)
        ratio = jnp.sqrt(old_mean + EPSILON) / jnp.sqrt(new_mean + EPSILON)
        w[m] = (updated * ratio).astype(BF)

    window_block(1)
    window_block(2)
    stage_two(order[0])
    window_block(3)
    stage_two(order[1])
    stage_two(order[2])
    halo.append(put(v_ref.at[pl.ds(TOK - WINDOW + 0, 64)], vx.at[pl.ds(0, 64)], following))
    stage_three(order[0])
    stage_three(order[1])
    stage_three(order[2])
    halo.append(put(v_ref.at[pl.ds(TOK - WINDOW + 64, 64)], vx.at[pl.ds(64, 64)], following))
    halo.append(put(v_ref.at[pl.ds(TOK - WINDOW + 128, 64)], vx.at[pl.ds(128, 64)], following))
    base = ((1 - zh) * 2 + core) * HD
    for m in order:
        stage_four(m)
    halo.append(put(v_ref.at[pl.ds(TOK - WINDOW + 192, 64)], vx.at[pl.ds(192, 64)], following))
    for m in order:
        stage_five(m)
    for m in order:
        stage_six(m)
    all_of(crossed)
    part_a = wo.at[pl.ds(aligned(base + row_a, 32), 32), pl.ds(0, 1024)]
    part_b = wo.at[pl.ds(aligned(base + row_b, 32), 32), pl.ds(1024, 1024)]
    spread = []
    for d in (1, 2, 3):
        spread.append(put(part_a, part_a, at_y(d)))
        spread.append(put(part_b, part_b, at_x(d)))
    own_core = [put(ow_ref, wo.at[own_rows], at_head(0, 1))]
    renew(0)
    all_of(spread)
    part_a = wo.at[pl.ds(aligned(base + x * 128, 128), 128), pl.ds(0, 1024)]
    part_b = wo.at[pl.ds(aligned(base + y * 128, 128), 128), pl.ds(1024, 1024)]
    renew(2)
    renew(1)
    spread = []
    for d in (1, 2, 3):
        spread.append(put(part_a, part_a, at_x(d)))
        spread.append(put(part_b, part_b, at_y(d)))

    all_of(halo)
    window_block(0)
    arrived = []
    for far, other in ((1, 0), (1, 1), (0, 1), (0, 0)):
        target = ((zh + far) % 2) * 2 + (core + other) % 2
        rows = pl.ds(aligned(target * 256, 256), 256)
        queries = qv[rows, :]
        gate = dotf(queries, w[0])
        up = dotf(queries, w[2])
        mixed = (gate * jax.nn.sigmoid(gate) * up).astype(BF)
        combined = (dotf(mixed, w[1]) + win[rows, :]).astype(BF)
        if far or other:
            cs[rows, :] = combined
            arrived.append((far, other, put(cs.at[rows], cr.at[h], at_head(far, other))))
        else:
            cr[h] = combined

    for copy in own_core + gain_got:
        copy.wait_recv()
    get_gain.wait()
    get_wo.wait()

    def project(far, other, fresh, squares):
        source = ((zh + far) % 2) * 2 + (core + other) % 2
        wide = cr[source].astype(F32)
        gain = gains[source].astype(F32)
        gain_row = jnp.concatenate([gain[i : i + 1, :] for i in range(4)], axis=1)
        squares = squares + jnp.sum(wide * wide, axis=1, keepdims=True)
        gained = (wide * gain_row).astype(BF)
        rows = pl.ds(aligned(source * HD, HD), HD)
        for n in range(4):
            cols = pl.ds(n * 512, 512)
            part = dotf(gained, wo[rows, cols])
            acc[:, cols] = part if fresh else acc[:, cols] + part
        return squares

    squares = project(0, 0, True, jnp.zeros((256, 1), F32))
    arrived[2][2].wait_recv()
    squares = project(0, 1, False, squares)
    for copy in spread:
        copy.wait_recv()
    far_rows = pl.ds(aligned(base, HD), HD)
    shared = put(wo.at[far_rows], wo.at[far_rows], at_head(0, 1))
    arrived[0][2].wait_recv()
    squares = project(1, 0, False, squares)
    arrived[1][2].wait_recv()
    shared.wait_recv()
    squares = project(1, 1, False, squares)
    scale = lax.rsqrt(squares * (1.0 / DM) + EPSILON)
    o_ref[...] = (acc[...] * scale).astype(BF)
    for copy in sends:
        copy.wait_send()


def body(queries, keys, values, rates, fast_w1, fast_w2, fast_w3, norm_gain, out_weight):
    anywhere = pl.BlockSpec(memory_space=pl.ANY)
    vmem = pl.BlockSpec(memory_space=pltpu.VMEM)
    n_copies = 128
    return pl.pallas_call(
        layer_kernel,
        out_shape=jax.ShapeDtypeStruct((TOK // 4, DM), BF),
        in_specs=[anywhere, anywhere, anywhere, vmem, anywhere, anywhere, anywhere, anywhere, anywhere],
        out_specs=vmem,
        scratch_shapes=[
            pltpu.VMEM((WINDOW + TOK, HD), BF),
            pltpu.VMEM((WINDOW + TOK, HD), BF),
            pltpu.VMEM((TOK, HD), BF),
            pltpu.VMEM((3, HD, HD), BF),
            pltpu.VMEM((TOK, 128), F32),
            pltpu.VMEM((TOK, HD), BF),
            pltpu.VMEM((TOK, HD), BF),
            pltpu.VMEM((TOK, HD), BF),
            pltpu.VMEM((TOK, HD), BF),
            pltpu.VMEM((3, HD, HD), BF),
            pltpu.VMEM((2, 3, 3, 128, 256), BF),
            pltpu.VMEM((2, 3, 128, 256), BF),
            pltpu.VMEM((2, 3, 3, 32, 256), BF),
            pltpu.VMEM((4, 3, 32, 128), BF),
            pltpu.VMEM((3, 3, 32, 128), BF),
            pltpu.VMEM((3, HD, HD), BF),
            pltpu.VMEM((8, HD), F32),
            pltpu.VMEM((TOK, HD), F32),
            pltpu.VMEM((DM, DM), BF),
            pltpu.VMEM((TOK, HD), BF),
            pltpu.VMEM((4, 256, HD), BF),
            pltpu.VMEM((256, DM), F32),
            pltpu.VMEM((4, 4, 128), BF),
            pltpu.SemaphoreType.DMA((n_copies,)),
            pltpu.SemaphoreType.DMA((n_copies,)),
            pltpu.SemaphoreType.DMA((8,)),
        ],
        name="layer",
        compiler_params=pltpu.CompilerParams(
            collective_id=0, has_side_effects=True, vmem_limit_bytes=60 << 20
        ),
    )(
        queries, keys, values, rates.reshape(8, 128),
        fast_w1[0], fast_w2[0], fast_w3[0], norm_gain.reshape(4, 128), out_weight,
    )


def solution(mesh):
    placed = (
        P("ctx", "head"),
        P("ctx", "head"),
        P("ctx", "head"),
        P("ctx", "head"),
        P("head", None, None),
        P("head", None, None),
        P("head", None, None),
        P("head"),
        P("head", None),
    )
    return jax.shard_map(
        body, mesh=mesh, in_specs=placed, out_specs=P(("ctx", "head"), None), check_vma=False
    )
```

```python
import math

import jax
import jax.numpy as jnp
from jax import lax
from jax.experimental import pallas as pl
from jax.experimental.pallas import tpu as pltpu
from jax.sharding import PartitionSpec as P

MESH = pl.DeviceIdType.MESH
WINDOW = 256
EPSILON = 1e-06
TOK = 1024
HD = 512
DM = 2048
NEG = -1e30
BF = jnp.bfloat16
F32 = jnp.float32


def dotf(a, b, ca=1, cb=0):
    return lax.dot_general(a, b, (((ca,), (cb,)), ((), ())), preferred_element_type=F32)


def device(zl, x, y, zh, core):
    return (zl * 16 + x * 4 + y, zh * 2 + core)


def aligned(value, by):
    return pl.multiple_of(value, by)


def layer_kernel(
    q_ref, k_ref, v_ref, rate_ref, w1_ref, w2_ref, w3_ref, gain_ref, ow_ref, o_ref,
    kx, vx, qv, w, rb, act, sc, g1, g3, ps, r1, q2, r2, q3, r3, f, asum, win, wo, cs, cr, acc, gains,
    send_sem, recv_sem, local_sem,
):
    c = lax.axis_index("ctx")
    h = lax.axis_index("head")
    zl, x, y = c // 16, (c // 4) % 4, c % 4
    zh, core = h // 2, h % 2

    def at_x(d):
        return device(zl, (x + d) % 4, y, zh, core)

    def at_y(d):
        return device(zl, x, (y + d) % 4, zh, core)

    def at_z(d):
        return device((zl + d) % 4, x, y, zh, core)

    def at_head(other_z, other_core):
        return device(
            zl, x, y, (zh + other_z) % 2, (core + other_core) % 2
        )

    following = ((c + 1) % 64, h)
    previous = ((c + 63) % 64, h)
    mirror = device(3 - zl, x, y, 1 - zh, core)
    used = [0]
    sends = []

    def put(src, dst, to):
        index = used[0]
        used[0] += 1
        copy = pltpu.make_async_remote_copy(
            src_ref=src, dst_ref=dst, send_sem=send_sem.at[index], recv_sem=recv_sem.at[index],
            device_id=to, device_id_type=MESH,
        )
        copy.start()
        sends.append(copy)
        return copy

    local = []

    def fetch(src, dst):
        copy = pltpu.make_async_copy(src, dst, local_sem.at[len(local)])
        copy.start()
        local.append(copy)
        return copy

    first = [
        fetch(k_ref, kx.at[pl.ds(WINDOW, TOK)]),
        fetch(w1_ref, w.at[0]),
        fetch(w3_ref, w.at[2]),
        fetch(v_ref, vx.at[pl.ds(WINDOW, TOK)]),
        fetch(w2_ref, w.at[1]),
    ]
    own_rows = pl.ds(aligned(h * HD, HD), HD)

    barrier = pltpu.get_barrier_semaphore()
    peers = [at_x(d) for d in (1, 2, 3)] + [at_y(d) for d in (1, 2, 3)] + [at_z(d) for d in (1, 2, 3)]
    peers += [at_head(0, 1), at_head(1, 0), at_head(1, 1), following, previous, mirror]
    for peer in peers:
        pl.semaphore_signal(barrier, inc=1, device_id=peer, device_id_type=MESH)

    pl.semaphore_wait(barrier, len(peers))

    tail = pl.ds(TOK - WINDOW, WINDOW)
    head = pl.ds(0, WINDOW)
    halo = [put(k_ref.at[tail], kx.at[head], following)]
    row_a = aligned(x * 128 + y * 32, 32)
    row_b = aligned(y * 128 + x * 32, 32)
    gain_got = [put(gain_ref, gains.at[h], at_head(a, b)) for a, b in ((0, 1), (1, 0), (1, 1))]
    for group in range(8):
        row = jnp.broadcast_to(rate_ref[group : group + 1, :], (128, 128))
        rb[group * 128 : (group + 1) * 128, :] = jnp.transpose(row)
    for copy in first:
        copy.wait()

    def token_block(i, carry):
        rows = pl.ds(aligned(i * 256, 256), 256)
        ext = pl.ds(aligned(i * 256 + WINDOW, 256), 256)
        key_rows = kx[ext, :]
        gate = dotf(key_rows, w[0])
        up = dotf(key_rows, w[2])
        sig = jax.nn.sigmoid(gate)
        gated = gate * sig
        act[rows, :] = (gated * up).astype(BF)
        rate = rb[rows, :]
        scaled = (vx[ext, :].astype(F32) * jnp.concatenate([rate] * 4, axis=1)).astype(BF)
        sc[rows, :] = scaled
        back = dotf(scaled, w[1], 1, 1)
        g1[rows, :] = (back * up * sig * (1.0 + gate * (1.0 - sig))).astype(BF)
        g3[rows, :] = (back * gated).astype(BF)
        return carry

    lax.fori_loop(0, TOK // 256, token_block, 0)
    get_q = fetch(q_ref, qv)
    get_wo = fetch(ow_ref, wo.at[own_rows])
    get_gain = fetch(gain_ref, gains.at[h])

    order = (0, 2, 1)
    own_keys = pl.ds(WINDOW, TOK)
    s1, s2, s3, s4, s5, s6 = {}, {}, {}, {}, {}, {}
    for m in order:
        for block in range(4):
            cols = pl.ds(block * 128, 128)
            left = act[:, cols] if m == 1 else kx[own_keys, cols]
            right = (g1, sc, g3)[m][...]
            ps[m, block * 128 : (block + 1) * 128, :] = dotf(left, right, 0, 0).astype(BF)
        s1[m] = []
        for d in (1, 2, 3):
            to_x = pl.ds(aligned(((x + d) % 4) * 128, 128), 128)
            to_y = pl.ds(aligned(((y + d) % 4) * 128, 128), 128)
            s1[m].append(put(ps.at[m, to_x, pl.ds(0, 256)], r1.at[0, d - 1, m], at_x(d)))
            s1[m].append(put(ps.at[m, to_y, pl.ds(256, 256)], r1.at[1, d - 1, m], at_y(d)))
    crossed = [
        put(
            ow_ref.at[pl.ds(row, 32), pl.ds(col, 1024)],
            wo.at[pl.ds(aligned(h * HD + row, 32), 32), pl.ds(col, 1024)],
            mirror,
        )
        for row, col in ((row_a, 0), (row_b, 1024))
    ]

    def window_block(b):
        queries = qv[b * 256 : (b + 1) * 256, :]
        scores = dotf(queries, kx[b * 256 : b * 256 + 512, :], 1, 1) * (1.0 / math.sqrt(HD))
        qi = lax.broadcasted_iota(jnp.int32, (256, 512), 0)
        ki = lax.broadcasted_iota(jnp.int32, (256, 512), 1)
        allowed = (ki <= qi + WINDOW) & (ki > qi)
        if b == 0:
            allowed = allowed & (ki >= jnp.where(c == 0, WINDOW, 0))
        scores = jnp.where(allowed, scores, NEG)
        peak = jnp.max(scores, axis=1, keepdims=True)
        expo = jnp.where(allowed, jnp.exp(scores - peak), 0.0)
        weights = (expo / jnp.sum(expo, axis=1, keepdims=True)).astype(BF)
        win[b * 256 : (b + 1) * 256, :] = dotf(weights, vx[b * 256 : b * 256 + 512, :])

    get_q.wait()
    for m in range(3):
        wide = w[m].astype(F32)
        asum[m : m + 1, :] = jnp.sum(wide * wide, axis=0, keepdims=True)

    def all_of(copies):
        for copy in copies:
            copy.wait_recv()

    def stage_two(m):
        all_of(s1[m])
        own_x = pl.ds(aligned(x * 128, 128), 128)
        own_y = pl.ds(aligned(y * 128, 128), 128)
        for half, own in ((0, own_x), (1, own_y)):
            total = ps[m, own, half * 256 : (half + 1) * 256].astype(F32)
            for d in range(3):
                total = total + r1[half, d, m].astype(F32)
            q2[half, m] = total.astype(BF)
        s2[m] = []
        for d in (1, 2, 3):
            to_y = pl.ds(aligned(((y + d) % 4) * 32, 32), 32)
            to_x = pl.ds(aligned(((x + d) % 4) * 32, 32), 32)
            s2[m].append(put(q2.at[0, m, to_y], r2.at[0, d - 1, m], at_y(d)))
            s2[m].append(put(q2.at[1, m, to_x], r2.at[1, d - 1, m], at_x(d)))

    def stage_three(m):
        all_of(s2[m])
        own_y = pl.ds(aligned(y * 32, 32), 32)
        own_x = pl.ds(aligned(x * 32, 32), 32)
        for half, own in ((0, own_y), (1, own_x)):
            total = q2[half, m, own, :].astype(F32)
            for d in range(3):
                total = total + r2[half, d, m].astype(F32)
            q3[2 * half, m] = total[:, :128].astype(BF)
            q3[2 * half + 1, m] = total[:, 128:].astype(BF)
        s3[m] = [put(q3.at[(zl + d) % 4, m], r3.at[d - 1, m], at_z(d)) for d in (1, 2, 3)]

    flip = zl // 2
    row_z = pl.ds(aligned((1 - flip) * row_a + flip * row_b, 32), 32)
    col_z = pl.ds(aligned(zl * 128, 128), 128)

    def stage_four(m):
        all_of(s3[m])
        total = q3[zl, m].astype(F32)
        for d in range(3):
            total = total + r3[d, m].astype(F32)
        f[m, row_z, col_z] = total.astype(BF)
        mine = f.at[m, row_z, col_z]
        s4[m] = [put(mine, mine, at_z(d)) for d in (1, 2, 3)]

    def stage_five(m):
        all_of(s4[m])
        part_a = f.at[m, pl.ds(row_a, 32), pl.ds(0, 256)]
        part_b = f.at[m, pl.ds(row_b, 32), pl.ds(256, 256)]
        s5[m] = []
        for d in (1, 2, 3):
            s5[m].append(put(part_a, part_a, at_y(d)))
            s5[m].append(put(part_b, part_b, at_x(d)))

    def stage_six(m):
        all_of(s5[m])
        part_a = f.at[m, pl.ds(aligned(x * 128, 128), 128), pl.ds(0, 256)]
        part_b = f.at[m, pl.ds(aligned(y * 128, 128), 128), pl.ds(256, 256)]
        s6[m] = []
        for d in (1, 2, 3):
            s6[m].append(put(part_a, part_a, at_x(d)))
            s6[m].append(put(part_b, part_b, at_y(d)))

    def renew(m):
        all_of(s6[m])
        updated = w[m].astype(F32) + f[m].astype(F32)
        new_mean = jnp.sum(updated * updated, axis=0, keepdims=True) * (1.0 / HD)
        old_mean = asum[m : m + 1, :] * (1.0 / HD)
        ratio = jnp.sqrt(old_mean + EPSILON) / jnp.sqrt(new_mean + EPSILON)
        w[m] = (updated * ratio).astype(BF)

    window_block(1)
    window_block(2)
    stage_two(order[0])
    window_block(3)
    stage_two(order[1])
    stage_two(order[2])
    halo.append(put(v_ref.at[pl.ds(TOK - WINDOW + 0, 64)], vx.at[pl.ds(0, 64)], following))
    stage_three(order[0])
    stage_three(order[1])
    stage_three(order[2])
    halo.append(put(v_ref.at[pl.ds(TOK - WINDOW + 64, 64)], vx.at[pl.ds(64, 64)], following))
    halo.append(put(v_ref.at[pl.ds(TOK - WINDOW + 128, 64)], vx.at[pl.ds(128, 64)], following))
    base = ((1 - zh) * 2 + core) * HD
    for m in order:
        stage_four(m)
    halo.append(put(v_ref.at[pl.ds(TOK - WINDOW + 192, 64)], vx.at[pl.ds(192, 64)], following))
    for m in order:
        stage_five(m)
    for m in order:
        stage_six(m)
    all_of(crossed)
    part_a = wo.at[pl.ds(aligned(base + row_a, 32), 32), pl.ds(0, 1024)]
    part_b = wo.at[pl.ds(aligned(base + row_b, 32), 32), pl.ds(1024, 1024)]
    spread = []
    for d in (1, 2, 3):
        spread.append(put(part_a, part_a, at_y(d)))
        spread.append(put(part_b, part_b, at_x(d)))
    own_core = [put(ow_ref, wo.at[own_rows], at_head(0, 1))]
    renew(0)
    all_of(spread)
    part_a = wo.at[pl.ds(aligned(base + x * 128, 128), 128), pl.ds(0, 1024)]
    part_b = wo.at[pl.ds(aligned(base + y * 128, 128), 128), pl.ds(1024, 1024)]
    renew(2)
    renew(1)
    spread = []
    for d in (1, 2, 3):
        spread.append(put(part_a, part_a, at_x(d)))
        spread.append(put(part_b, part_b, at_y(d)))

    all_of(halo)
    window_block(0)
    arrived = []
    for far, other in ((1, 0), (1, 1), (0, 1), (0, 0)):
        target = ((zh + far) % 2) * 2 + (core + other) % 2
        rows = pl.ds(aligned(target * 256, 256), 256)
        queries = qv[rows, :]
        gate = dotf(queries, w[0])
        up = dotf(queries, w[2])
        mixed = (gate * jax.nn.sigmoid(gate) * up).astype(BF)
        combined = (dotf(mixed, w[1]) + win[rows, :]).astype(BF)
        if far or other:
            cs[rows, :] = combined
            arrived.append((far, other, put(cs.at[rows], cr.at[h], at_head(far, other))))
        else:
            cr[h] = combined

    for copy in own_core + gain_got:
        copy.wait_recv()
    get_gain.wait()
    get_wo.wait()

    def project(far, other, fresh, squares):
        source = ((zh + far) % 2) * 2 + (core + other) % 2
        wide = cr[source].astype(F32)
        gain = gains[source].astype(F32)
        gain_row = jnp.concatenate([gain[i : i + 1, :] for i in range(4)], axis=1)
        squares = squares + jnp.sum(wide * wide, axis=1, keepdims=True)
        gained = (wide * gain_row).astype(BF)
        rows = pl.ds(aligned(source * HD, HD), HD)
        for n in range(4):
            cols = pl.ds(n * 512, 512)
            part = dotf(gained, wo[rows, cols])
            acc[:, cols] = part if fresh else acc[:, cols] + part
        return squares

    squares = project(0, 0, True, jnp.zeros((256, 1), F32))
    arrived[2][2].wait_recv()
    squares = project(0, 1, False, squares)
    for copy in spread:
        copy.wait_recv()
    far_rows = pl.ds(aligned(base, HD), HD)
    shared = put(wo.at[far_rows], wo.at[far_rows], at_head(0, 1))
    arrived[0][2].wait_recv()
    squares = project(1, 0, False, squares)
    arrived[1][2].wait_recv()
    shared.wait_recv()
    squares = project(1, 1, False, squares)
    scale = lax.rsqrt(squares * (1.0 / DM) + EPSILON)
    o_ref[...] = (acc[...] * scale).astype(BF)
    for copy in sends:
        copy.wait_send()


def body(queries, keys, values, rates, fast_w1, fast_w2, fast_w3, norm_gain, out_weight):
    anywhere = pl.BlockSpec(memory_space=pl.ANY)
    vmem = pl.BlockSpec(memory_space=pltpu.VMEM)
    n_copies = 128
    return pl.pallas_call(
        layer_kernel,
        out_shape=jax.ShapeDtypeStruct((TOK // 4, DM), BF),
        in_specs=[anywhere, anywhere, anywhere, vmem, anywhere, anywhere, anywhere, anywhere, anywhere],
        out_specs=vmem,
        scratch_shapes=[
            pltpu.VMEM((WINDOW + TOK, HD), BF),
            pltpu.VMEM((WINDOW + TOK, HD), BF),
            pltpu.VMEM((TOK, HD), BF),
            pltpu.VMEM((3, HD, HD), BF),
            pltpu.VMEM((TOK, 128), F32),
            pltpu.VMEM((TOK, HD), BF),
            pltpu.VMEM((TOK, HD), BF),
            pltpu.VMEM((TOK, HD), BF),
            pltpu.VMEM((TOK, HD), BF),
            pltpu.VMEM((3, HD, HD), BF),
            pltpu.VMEM((2, 3, 3, 128, 256), BF),
            pltpu.VMEM((2, 3, 128, 256), BF),
            pltpu.VMEM((2, 3, 3, 32, 256), BF),
            pltpu.VMEM((4, 3, 32, 128), BF),
            pltpu.VMEM((3, 3, 32, 128), BF),
            pltpu.VMEM((3, HD, HD), BF),
            pltpu.VMEM((8, HD), F32),
            pltpu.VMEM((TOK, HD), F32),
            pltpu.VMEM((DM, DM), BF),
            pltpu.VMEM((TOK, HD), BF),
            pltpu.VMEM((4, 256, HD), BF),
            pltpu.VMEM((256, DM), F32),
            pltpu.VMEM((4, 4, 128), BF),
            pltpu.SemaphoreType.DMA((n_copies,)),
            pltpu.SemaphoreType.DMA((n_copies,)),
            pltpu.SemaphoreType.DMA((8,)),
        ],
        name="layer",
        compiler_params=pltpu.CompilerParams(
            collective_id=0, has_side_effects=True, vmem_limit_bytes=60 << 20
        ),
    )(
        queries, keys, values, rates.reshape(8, 128),
        fast_w1[0], fast_w2[0], fast_w3[0], norm_gain.reshape(4, 128), out_weight,
    )


def solution(mesh):
    placed = (
        P("ctx", "head"),
        P("ctx", "head"),
        P("ctx", "head"),
        P("ctx", "head"),
        P("head", None, None),
        P("head", None, None),
        P("head", None, None),
        P("head"),
        P("head", None),
    )
    return jax.shard_map(
        body, mesh=mesh, in_specs=placed, out_specs=P(("ctx", "head"), None), check_vma=False
    )
```

```python
import math

import jax
import jax.numpy as jnp
from jax import lax
from jax.experimental import pallas as pl
from jax.experimental.pallas import tpu as pltpu
from jax.sharding import PartitionSpec as P

MESH = pl.DeviceIdType.MESH
WINDOW = 256
EPSILON = 1e-06
TOK = 1024
HD = 512
DM = 2048
NEG = -1e30
BF = jnp.bfloat16
F32 = jnp.float32


def dotf(a, b, ca=1, cb=0):
    return lax.dot_general(a, b, (((ca,), (cb,)), ((), ())), preferred_element_type=F32)


def device(zl, x, y, zh, core):
    return (zl * 16 + x * 4 + y, zh * 2 + core)


def aligned(value, by):
    return pl.multiple_of(value, by)


def layer_kernel(
    q_ref, k_ref, v_ref, rate_ref, w1_ref, w2_ref, w3_ref, gain_ref, ow_ref, o_ref,
    kx, vx, qv, w, rb, act, sc, g1, g3, ps, r1, q2, r2, q3, r3, f, asum, win, wo, cs, cr, acc, gains,
    send_sem, recv_sem, local_sem,
):
    c = lax.axis_index("ctx")
    h = lax.axis_index("head")
    zl, x, y = c // 16, (c // 4) % 4, c % 4
    zh, core = h // 2, h % 2

    def at_x(d):
        return device(zl, (x + d) % 4, y, zh, core)

    def at_y(d):
        return device(zl, x, (y + d) % 4, zh, core)

    def at_z(d):
        return device((zl + d) % 4, x, y, zh, core)

    def at_head(other_z, other_core):
        return device(
            zl, x, y, (zh + other_z) % 2, (core + other_core) % 2
        )

    following = ((c + 1) % 64, h)
    previous = ((c + 63) % 64, h)
    mirror = device(3 - zl, x, y, 1 - zh, core)
    used = [0]
    sends = []

    def put(src, dst, to):
        index = used[0]
        used[0] += 1
        copy = pltpu.make_async_remote_copy(
            src_ref=src, dst_ref=dst, send_sem=send_sem.at[index], recv_sem=recv_sem.at[index],
            device_id=to, device_id_type=MESH,
        )
        copy.start()
        sends.append(copy)
        return copy

    local = []

    def fetch(src, dst):
        copy = pltpu.make_async_copy(src, dst, local_sem.at[len(local)])
        copy.start()
        local.append(copy)
        return copy

    first = [
        fetch(k_ref, kx.at[pl.ds(WINDOW, TOK)]),
        fetch(w1_ref, w.at[0]),
        fetch(w3_ref, w.at[2]),
        fetch(v_ref, vx.at[pl.ds(WINDOW, TOK)]),
        fetch(w2_ref, w.at[1]),
    ]
    own_rows = pl.ds(aligned(h * HD, HD), HD)

    barrier = pltpu.get_barrier_semaphore()
    peers = [at_x(d) for d in (1, 2, 3)] + [at_y(d) for d in (1, 2, 3)] + [at_z(d) for d in (1, 2, 3)]
    peers += [at_head(0, 1), at_head(1, 0), at_head(1, 1), following, previous, mirror]
    for peer in peers:
        pl.semaphore_signal(barrier, inc=1, device_id=peer, device_id_type=MESH)

    pl.semaphore_wait(barrier, len(peers))

    tail = pl.ds(TOK - WINDOW, WINDOW)
    head = pl.ds(0, WINDOW)
    halo = [put(k_ref.at[tail], kx.at[head], following)]
    row_a = aligned(x * 128 + y * 32, 32)
    row_b = aligned(y * 128 + x * 32, 32)
    gain_got = [put(gain_ref, gains.at[h], at_head(a, b)) for a, b in ((0, 1), (1, 0), (1, 1))]
    for group in range(8):
        row = jnp.broadcast_to(rate_ref[group : group + 1, :], (128, 128))
        rb[group * 128 : (group + 1) * 128, :] = jnp.transpose(row)
    for copy in first:
        copy.wait()

    def token_block(i, carry):
        rows = pl.ds(aligned(i * 256, 256), 256)
        ext = pl.ds(aligned(i * 256 + WINDOW, 256), 256)
        key_rows = kx[ext, :]
        gate = dotf(key_rows, w[0])
        up = dotf(key_rows, w[2])
        sig = jax.nn.sigmoid(gate)
        gated = gate * sig
        act[rows, :] = (gated * up).astype(BF)
        rate = rb[rows, :]
        scaled = (vx[ext, :].astype(F32) * jnp.concatenate([rate] * 4, axis=1)).astype(BF)
        sc[rows, :] = scaled
        back = dotf(scaled, w[1], 1, 1)
        g1[rows, :] = (back * up * sig * (1.0 + gate * (1.0 - sig))).astype(BF)
        g3[rows, :] = (back * gated).astype(BF)
        return carry

    lax.fori_loop(0, TOK // 256, token_block, 0)
    get_q = fetch(q_ref, qv)
    get_wo = fetch(ow_ref, wo.at[own_rows])
    get_gain = fetch(gain_ref, gains.at[h])

    order = (0, 2, 1)
    own_keys = pl.ds(WINDOW, TOK)
    s1, s2, s3, s4, s5, s6 = {}, {}, {}, {}, {}, {}
    for m in order:
        for block in range(4):
            cols = pl.ds(block * 128, 128)
            left = act[:, cols] if m == 1 else kx[own_keys, cols]
            right = (g1, sc, g3)[m][...]
            ps[m, block * 128 : (block + 1) * 128, :] = dotf(left, right, 0, 0).astype(BF)
        s1[m] = []
        for d in (1, 2, 3):
            to_x = pl.ds(aligned(((x + d) % 4) * 128, 128), 128)
            to_y = pl.ds(aligned(((y + d) % 4) * 128, 128), 128)
            s1[m].append(put(ps.at[m, to_x, pl.ds(0, 256)], r1.at[0, d - 1, m], at_x(d)))
            s1[m].append(put(ps.at[m, to_y, pl.ds(256, 256)], r1.at[1, d - 1, m], at_y(d)))
    crossed = [
        put(
            ow_ref.at[pl.ds(row, 32), pl.ds(col, 1024)],
            wo.at[pl.ds(aligned(h * HD + row, 32), 32), pl.ds(col, 1024)],
            mirror,
        )
        for row, col in ((row_a, 0), (row_b, 1024))
    ]

    def window_block(b):
        queries = qv[b * 256 : (b + 1) * 256, :]
        scores = dotf(queries, kx[b * 256 : b * 256 + 512, :], 1, 1) * (1.0 / math.sqrt(HD))
        qi = lax.broadcasted_iota(jnp.int32, (256, 512), 0)
        ki = lax.broadcasted_iota(jnp.int32, (256, 512), 1)
        allowed = (ki <= qi + WINDOW) & (ki > qi)
        if b == 0:
            allowed = allowed & (ki >= jnp.where(c == 0, WINDOW, 0))
        scores = jnp.where(allowed, scores, NEG)
        peak = jnp.max(scores, axis=1, keepdims=True)
        expo = jnp.where(allowed, jnp.exp(scores - peak), 0.0)
        weights = (expo / jnp.sum(expo, axis=1, keepdims=True)).astype(BF)
        win[b * 256 : (b + 1) * 256, :] = dotf(weights, vx[b * 256 : b * 256 + 512, :])

    get_q.wait()
    for m in range(3):
        wide = w[m].astype(F32)
        asum[m : m + 1, :] = jnp.sum(wide * wide, axis=0, keepdims=True)

    def all_of(copies):
        for copy in copies:
            copy.wait_recv()

    def stage_two(m):
        all_of(s1[m])
        own_x = pl.ds(aligned(x * 128, 128), 128)
        own_y = pl.ds(aligned(y * 128, 128), 128)
        for half, own in ((0, own_x), (1, own_y)):
            total = ps[m, own, half * 256 : (half + 1) * 256].astype(F32)
            for d in range(3):
                total = total + r1[half, d, m].astype(F32)
            q2[half, m] = total.astype(BF)
        s2[m] = []
        for d in (1, 2, 3):
            to_y = pl.ds(aligned(((y + d) % 4) * 32, 32), 32)
            to_x = pl.ds(aligned(((x + d) % 4) * 32, 32), 32)
            s2[m].append(put(q2.at[0, m, to_y], r2.at[0, d - 1, m], at_y(d)))
            s2[m].append(put(q2.at[1, m, to_x], r2.at[1, d - 1, m], at_x(d)))

    def stage_three(m):
        all_of(s2[m])
        own_y = pl.ds(aligned(y * 32, 32), 32)
        own_x = pl.ds(aligned(x * 32, 32), 32)
        for half, own in ((0, own_y), (1, own_x)):
            total = q2[half, m, own, :].astype(F32)
            for d in range(3):
                total = total + r2[half, d, m].astype(F32)
            q3[2 * half, m] = total[:, :128].astype(BF)
            q3[2 * half + 1, m] = total[:, 128:].astype(BF)
        s3[m] = [put(q3.at[(zl + d) % 4, m], r3.at[d - 1, m], at_z(d)) for d in (1, 2, 3)]

    flip = zl // 2
    row_z = pl.ds(aligned((1 - flip) * row_a + flip * row_b, 32), 32)
    col_z = pl.ds(aligned(zl * 128, 128), 128)

    def stage_four(m):
        all_of(s3[m])
        total = q3[zl, m].astype(F32)
        for d in range(3):
            total = total + r3[d, m].astype(F32)
        f[m, row_z, col_z] = total.astype(BF)
        mine = f.at[m, row_z, col_z]
        s4[m] = [put(mine, mine, at_z(d)) for d in (1, 2, 3)]

    def stage_five(m):
        all_of(s4[m])
        part_a = f.at[m, pl.ds(row_a, 32), pl.ds(0, 256)]
        part_b = f.at[m, pl.ds(row_b, 32), pl.ds(256, 256)]
        s5[m] = []
        for d in (1, 2, 3):
            s5[m].append(put(part_a, part_a, at_y(d)))
            s5[m].append(put(part_b, part_b, at_x(d)))

    def stage_six(m):
        all_of(s5[m])
        part_a = f.at[m, pl.ds(aligned(x * 128, 128), 128), pl.ds(0, 256)]
        part_b = f.at[m, pl.ds(aligned(y * 128, 128), 128), pl.ds(256, 256)]
        s6[m] = []
        for d in (1, 2, 3):
            s6[m].append(put(part_a, part_a, at_x(d)))
            s6[m].append(put(part_b, part_b, at_y(d)))

    def renew(m):
        all_of(s6[m])
        updated = w[m].astype(F32) + f[m].astype(F32)
        new_mean = jnp.sum(updated * updated, axis=0, keepdims=True) * (1.0 / HD)
        old_mean = asum[m : m + 1, :] * (1.0 / HD)
        ratio = jnp.sqrt(old_mean + EPSILON) / jnp.sqrt(new_mean + EPSILON)
        w[m] = (updated * ratio).astype(BF)

    window_block(1)
    window_block(2)
    stage_two(order[0])
    window_block(3)
    stage_two(order[1])
    stage_two(order[2])
    halo.append(put(v_ref.at[pl.ds(TOK - WINDOW + 0, 64)], vx.at[pl.ds(0, 64)], following))
    stage_three(order[0])
    stage_three(order[1])
    stage_three(order[2])
    halo.append(put(v_ref.at[pl.ds(TOK - WINDOW + 64, 64)], vx.at[pl.ds(64, 64)], following))
    halo.append(put(v_ref.at[pl.ds(TOK - WINDOW + 128, 64)], vx.at[pl.ds(128, 64)], following))
    base = ((1 - zh) * 2 + core) * HD
    for m in order:
        stage_four(m)
    halo.append(put(v_ref.at[pl.ds(TOK - WINDOW + 192, 64)], vx.at[pl.ds(192, 64)], following))
    for m in order:
        stage_five(m)
    for m in order:
        stage_six(m)
    all_of(crossed)
    part_a = wo.at[pl.ds(aligned(base + row_a, 32), 32), pl.ds(0, 1024)]
    part_b = wo.at[pl.ds(aligned(base + row_b, 32), 32), pl.ds(1024, 1024)]
    spread = []
    for d in (1, 2, 3):
        spread.append(put(part_a, part_a, at_y(d)))
        spread.append(put(part_b, part_b, at_x(d)))
    renew(0)
    all_of(spread)
    part_a = wo.at[pl.ds(aligned(base + x * 128, 128), 128), pl.ds(0, 1024)]
    part_b = wo.at[pl.ds(aligned(base + y * 128, 128), 128), pl.ds(1024, 1024)]
    renew(2)
    renew(1)
    spread = []
    for d in (1, 2, 3):
        spread.append(put(part_a, part_a, at_x(d)))
        spread.append(put(part_b, part_b, at_y(d)))

    all_of(halo)
    window_block(0)
    arrived = []
    for far, other in ((1, 0), (1, 1), (0, 1), (0, 0)):
        target = ((zh + far) % 2) * 2 + (core + other) % 2
        rows = pl.ds(aligned(target * 256, 256), 256)
        queries = qv[rows, :]
        gate = dotf(queries, w[0])
        up = dotf(queries, w[2])
        mixed = (gate * jax.nn.sigmoid(gate) * up).astype(BF)
        combined = (dotf(mixed, w[1]) + win[rows, :]).astype(BF)
        if far or other:
            cs[rows, :] = combined
            arrived.append((far, other, put(cs.at[rows], cr.at[h], at_head(far, other))))
        else:
            cr[h] = combined

    own_core = [put(ow_ref, wo.at[own_rows], at_head(0, 1))]
    for copy in own_core + gain_got:
        copy.wait_recv()
    get_gain.wait()
    get_wo.wait()

    def project(far, other, fresh, squares):
        source = ((zh + far) % 2) * 2 + (core + other) % 2
        wide = cr[source].astype(F32)
        gain = gains[source].astype(F32)
        gain_row = jnp.concatenate([gain[i : i + 1, :] for i in range(4)], axis=1)
        squares = squares + jnp.sum(wide * wide, axis=1, keepdims=True)
        gained = (wide * gain_row).astype(BF)
        rows = pl.ds(aligned(source * HD, HD), HD)
        for n in range(4):
            cols = pl.ds(n * 512, 512)
            part = dotf(gained, wo[rows, cols])
            acc[:, cols] = part if fresh else acc[:, cols] + part
        return squares

    squares = project(0, 0, True, jnp.zeros((256, 1), F32))
    arrived[2][2].wait_recv()
    squares = project(0, 1, False, squares)
    for copy in spread:
        copy.wait_recv()
    far_rows = pl.ds(aligned(base, HD), HD)
    shared = put(wo.at[far_rows], wo.at[far_rows], at_head(0, 1))
    arrived[0][2].wait_recv()
    squares = project(1, 0, False, squares)
    arrived[1][2].wait_recv()
    shared.wait_recv()
    squares = project(1, 1, False, squares)
    scale = lax.rsqrt(squares * (1.0 / DM) + EPSILON)
    o_ref[...] = (acc[...] * scale).astype(BF)
    for copy in sends:
        copy.wait_send()


def body(queries, keys, values, rates, fast_w1, fast_w2, fast_w3, norm_gain, out_weight):
    anywhere = pl.BlockSpec(memory_space=pl.ANY)
    vmem = pl.BlockSpec(memory_space=pltpu.VMEM)
    n_copies = 128
    return pl.pallas_call(
        layer_kernel,
        out_shape=jax.ShapeDtypeStruct((TOK // 4, DM), BF),
        in_specs=[anywhere, anywhere, anywhere, vmem, anywhere, anywhere, anywhere, anywhere, anywhere],
        out_specs=vmem,
        scratch_shapes=[
            pltpu.VMEM((WINDOW + TOK, HD), BF),
            pltpu.VMEM((WINDOW + TOK, HD), BF),
            pltpu.VMEM((TOK, HD), BF),
            pltpu.VMEM((3, HD, HD), BF),
            pltpu.VMEM((TOK, 128), F32),
            pltpu.VMEM((TOK, HD), BF),
            pltpu.VMEM((TOK, HD), BF),
            pltpu.VMEM((TOK, HD), BF),
            pltpu.VMEM((TOK, HD), BF),
            pltpu.VMEM((3, HD, HD), BF),
            pltpu.VMEM((2, 3, 3, 128, 256), BF),
            pltpu.VMEM((2, 3, 128, 256), BF),
            pltpu.VMEM((2, 3, 3, 32, 256), BF),
            pltpu.VMEM((4, 3, 32, 128), BF),
            pltpu.VMEM((3, 3, 32, 128), BF),
            pltpu.VMEM((3, HD, HD), BF),
            pltpu.VMEM((8, HD), F32),
            pltpu.VMEM((TOK, HD), F32),
            pltpu.VMEM((DM, DM), BF),
            pltpu.VMEM((TOK, HD), BF),
            pltpu.VMEM((4, 256, HD), BF),
            pltpu.VMEM((256, DM), F32),
            pltpu.VMEM((4, 4, 128), BF),
            pltpu.SemaphoreType.DMA((n_copies,)),
            pltpu.SemaphoreType.DMA((n_copies,)),
            pltpu.SemaphoreType.DMA((8,)),
        ],
        name="layer",
        compiler_params=pltpu.CompilerParams(
            collective_id=0, has_side_effects=True, vmem_limit_bytes=60 << 20
        ),
    )(
        queries, keys, values, rates.reshape(8, 128),
        fast_w1[0], fast_w2[0], fast_w3[0], norm_gain.reshape(4, 128), out_weight,
    )


def solution(mesh):
    placed = (
        P("ctx", "head"),
        P("ctx", "head"),
        P("ctx", "head"),
        P("ctx", "head"),
        P("head", None, None),
        P("head", None, None),
        P("head", None, None),
        P("head"),
        P("head", None),
    )
    return jax.shard_map(
        body, mesh=mesh, in_specs=placed, out_specs=P(("ctx", "head"), None), check_vma=False
    )
```
